256 devices in a mesh: vp: 32 (over x, z), vc: 8 (over y, core).
Axes of the slice: x: 4, y: 4, z: 8, core: 2. Of those that a mesh axis runs over, the one named last changes fastest.
Arguments:
- amplitudes: bfloat16 [512, 204800], P(('vp', 'vc')), may hold values from -6 to 6
- pair_tiles: bfloat16 [65536, 128, 128], P(('vp', 'vc')), may hold values from -0.0625 to 0.0625
- slot_pairs: int32 [65536, 2], P(('vp', 'vc')), may hold values from 0 to 199, as said below
- slot_count: int32 [256], P(('vp', 'vc')), may hold values from 32 to 256, as said below
Outputs:
- ladder: bfloat16 [512, 65536], P('vc', 'vp')
The draws below stay inside these ranges and needn't reach their ends.
Inputs may be any that keep to these rules, and one draw needn't show every extreme that they name: `slot_pairs`: the rows of one device name distinct pairs; column 0 lies in 0 to 15, column 1 in 0 to 199. `slot_count`: every count is 256 divided by 1, 2, 4 or 8; some device has exactly 256.
All inputs are finite; a program needn't handle non-finite values.
Results may differ from the reference program's by a relative error of at most 0.001.
Values may be sent and summed in bfloat16 or wider, within the bound.
No kernel may reach another device: no remote copies, remote signals or barrier semaphores. Data moves between devices by JAX's collectives and lax.ppermute only.
A program may use at most 128 MiB of HBM per device.

```python
import jax
import jax.numpy as jnp
from jax import lax

TILE = 128
ABT_DEV = 16
CT_DEV = 200
SLOTS_DEV = 256
PAIRS = 512
CD = 204800
AB = 65536
ALL_SLOTS = 65536
N_VP = 32
N_VC = 8


def draw_slot_pairs(key, part):
    device_keys = jax.random.split(jax.random.fold_in(key, 11), N_VP * N_VC)

    def one_device(device_key):
        shuffled = jax.random.permutation(device_key, ABT_DEV * CT_DEV)[:SLOTS_DEV]
        return jnp.stack([shuffled // CT_DEV, shuffled % CT_DEV], axis=1)
    return jax.vmap(one_device)(device_keys).reshape(N_VP * N_VC * SLOTS_DEV, 2).astype(jnp.int32)


def draw_slot_count(key, part):
    device_total = N_VP * N_VC
    halvings = jax.random.randint(jax.random.fold_in(key, 21), (device_total,), 0, 4)
    counts = jnp.right_shift(jnp.full((device_total,), SLOTS_DEV, jnp.int32), halvings.astype(jnp.int32))
    chosen = jax.random.randint(jax.random.fold_in(key, 22), (), 0, device_total)
    counts = jnp.where(jnp.arange(device_total) == chosen, SLOTS_DEV, counts)
    return counts.astype(jnp.int32)


def levels(own_key, shape, shards, smallest, high):
    gain = 1.0
    for position, blocks in shards:
        draws = jax.random.uniform(jax.random.fold_in(jax.random.fold_in(own_key, 6), position), (blocks,), jnp.float32, smallest / len(shards), high / len(shards))
        gain = gain * jnp.repeat(jnp.exp(draws), shape[position] // blocks).reshape((-1,) + (1,) * (len(shape) - 1 - position))
    return gain


def scatter_about(key, extent, deviation, bound, shards=(), kind=jnp.bfloat16):
    result = jax.random.normal(key, extent, jnp.float32) * deviation
    if len(shards) > 0:
        result = levels(key, extent, shards, -0.22, 0.18) * result
    return jnp.clip(result, min=-bound, max=bound).astype(kind)


def setup_inputs(seed: int = 0) -> dict:
    arg_keys = jax.random.split(jax.random.key(seed), 5)
    return {
        "amplitudes": scatter_about(arg_keys[0], (PAIRS, CD), 1.0, 6.0, ((0, 256),)),
        "pair_tiles": scatter_about(arg_keys[1], (ALL_SLOTS, TILE, TILE), (SLOTS_DEV * TILE * N_VC // (2 * ABT_DEV)) ** -0.5, 0.0625, ((0, 256),)),
        "slot_pairs": draw_slot_pairs(jax.random.fold_in(arg_keys[4], 71), 0),
        "slot_count": draw_slot_count(jax.random.fold_in(arg_keys[4], 71), 0),
    }


def reference(amplitudes, pair_tiles, slot_pairs, slot_count):
    device_total = N_VP * N_VC
    grouped = amplitudes.astype(jnp.float32).reshape(PAIRS, CT_DEV * N_VC, TILE)
    all_tiles = pair_tiles.reshape(device_total, SLOTS_DEV, TILE, TILE)
    all_pairs = slot_pairs.reshape(device_total, SLOTS_DEV, 2)

    def add_device(totals, inputs):
        device_index, tiles_block, slot_table, live_count = inputs
        row_block = device_index // N_VC
        col_block = device_index % N_VC
        cd_index = (col_block * CT_DEV + slot_table[:, 1]).astype(jnp.int32)
        picked = jnp.take(grouped, cd_index, axis=1)
        product = jnp.einsum('pkc,kcn->pkn', picked, tiles_block.astype(jnp.float32), precision=lax.Precision.HIGHEST)
        alive_mask = (jnp.arange(SLOTS_DEV, dtype=jnp.int32) < live_count).astype(jnp.float32)
        select = (slot_table[:, 0][:, None] == jnp.arange(ABT_DEV, dtype=jnp.int32)[None, :]).astype(jnp.float32) * alive_mask[:, None]
        block_sum = jnp.einsum('pkn,ka->pan', product, select, precision=lax.Precision.HIGHEST)
        offset_tile = (row_block * ABT_DEV).astype(jnp.int32)
        current = lax.dynamic_slice_in_dim(totals, offset_tile, ABT_DEV, 1)
        totals = lax.dynamic_update_slice_in_dim(totals, current + block_sum, offset_tile, 1)
        return totals, None

    start_totals = jnp.zeros((PAIRS, ABT_DEV * N_VP, TILE), jnp.float32)
    totals, unused = lax.scan(add_device, start_totals, (jnp.arange(device_total, dtype=jnp.int32), all_tiles, all_pairs, slot_count))
    return totals.reshape(PAIRS, AB).astype(jnp.bfloat16)
```

```python
import jax
import jax.numpy as jnp
from jax import lax
from jax.experimental import pallas as pl
from jax.experimental.pallas import tpu as pltpu
from jax.sharding import PartitionSpec as P

TILE = 128
AB_TILES = 16
GROUP = 4


def plan_kernel(slots, entries, groups, ab_ref, cd_ref, count_ref, c_ref, s_ref, a_ref, n_ref, next_ref):
    live = count_ref[0]

    def clear(i, _):
        next_ref[i] = 0
        return 0

    lax.fori_loop(0, AB_TILES, clear, 0)

    def count(i, _):
        a = ab_ref[i]
        next_ref[a] = next_ref[a] + 1
        return 0

    lax.fori_loop(0, live, count, 0)

    def blank(i, _):
        c_ref[i] = 0
        s_ref[i] = slots
        return 0

    lax.fori_loop(0, entries, blank, 0)

    def place(a, first):
        n = (next_ref[a] + GROUP - 1) // GROUP
        next_ref[a] = first * GROUP

        def mark(g, _):
            a_ref[first + g] = a
            return 0

        lax.fori_loop(0, n, mark, 0)
        return first + n

    n_ref[0] = lax.fori_loop(0, AB_TILES, place, 0)

    def fill(i, _):
        a = ab_ref[i]
        e = next_ref[a]
        c_ref[e] = cd_ref[i]
        s_ref[e] = i
        next_ref[a] = e + 1
        return 0

    lax.fori_loop(0, live, fill, 0)


def make_plan(ab, cd, count):
    slots = ab.shape[0]
    groups = slots // GROUP + AB_TILES
    entries = groups * GROUP
    smem = pl.BlockSpec(memory_space=pltpu.SMEM)
    ints = lambda n: jax.ShapeDtypeStruct((n,), jnp.int32)
    return pl.pallas_call(
        lambda *refs: plan_kernel(slots, entries, groups, *refs),
        out_shape=(ints(entries), ints(entries), ints(groups), ints(1)),
        in_specs=[smem] * 3,
        out_specs=(smem,) * 4,
        scratch_shapes=[pltpu.SMEM((AB_TILES,), jnp.int32)],
        name="plan",
    )(ab, cd, count)


def contract_kernel(c_ref, s_ref, a_ref, n_ref, rows_hbm, tiles_hbm, out_ref, rows, tiles, sems):
    slots = tiles_hbm.shape[0]
    columns = rows.shape[0]
    tiles_copy = pltpu.make_async_copy(tiles_hbm, tiles.at[pl.ds(0, slots)], sems.at[0])
    tiles_copy.start()

    def fetch(c, _):
        pltpu.make_async_copy(
            rows_hbm.at[:, pl.ds(pl.multiple_of(c * TILE, TILE), TILE)], rows.at[c], sems.at[1]
        ).start()
        return 0

    lax.fori_loop(0, columns, fetch, 0)
    tiles[slots] = jnp.zeros((TILE, TILE), tiles.dtype)
    out_ref[...] = jnp.zeros_like(out_ref)
    tiles_copy.wait()
    pltpu.make_async_copy(rows, rows, sems.at[1]).wait()

    def step(g, _):
        e = g * GROUP
        lhs = jnp.concatenate([rows[c_ref[e + k]] for k in range(GROUP)], axis=1)
        rhs = jnp.concatenate([tiles[s_ref[e + k]] for k in range(GROUP)], axis=0)
        where = pl.ds(pl.multiple_of(a_ref[g] * TILE, TILE), TILE)
        out_ref[:, where] += jnp.dot(lhs, rhs, preferred_element_type=jnp.float32)
        return 0

    lax.fori_loop(0, n_ref[0], step, 0)


def contract(rows, tiles, plan):
    height, width = rows.shape
    slots = tiles.shape[0]
    smem = pl.BlockSpec(memory_space=pltpu.SMEM)
    hbm = pl.BlockSpec(memory_space=pl.ANY)
    out_width = AB_TILES * TILE
    return pl.pallas_call(
        contract_kernel,
        out_shape=jax.ShapeDtypeStruct((height, out_width), jnp.float32),
        in_specs=[smem] * 4 + [hbm] * 2,
        out_specs=pl.BlockSpec(memory_space=pltpu.VMEM),
        scratch_shapes=[
            pltpu.VMEM((width // TILE, height, TILE), rows.dtype),
            pltpu.VMEM((slots + 1, TILE, TILE), tiles.dtype),
            pltpu.SemaphoreType.DMA((2,)),
        ],
        compiler_params=pltpu.CompilerParams(vmem_limit_bytes=40 * 1024 * 1024),
        cost_estimate=pl.CostEstimate(
            flops=2 * height * slots * TILE * TILE,
            bytes_accessed=2 * height * width + 2 * slots * TILE * TILE + 4 * height * out_width,
            transcendentals=0,
        ),
        name="contract",
    )(*plan, rows, tiles)


def per_device(amplitudes, pair_tiles, slot_pairs, slot_count):
    plan = make_plan(slot_pairs[:, 0], slot_pairs[:, 1], slot_count)
    n_vc = 8
    parts = []
    for h in range(2):
        own = amplitudes[h : h + 1].reshape(n_vc, -1)
        block = lax.all_to_all(own, "vc", split_axis=0, concat_axis=0, tiled=True)
        rows = lax.all_gather(block, "vp", axis=0, tiled=True)
        partial = contract(rows, pair_tiles, plan)
        parts.append(lax.psum_scatter(partial, "vc", scatter_dimension=0, tiled=True))
    width = parts[0].shape[1]
    joined = jnp.stack([p.reshape(-1, n_vc, width) for p in parts], axis=2)
    return joined.reshape(-1, width).astype(jnp.bfloat16)


def solution(mesh):
    in_specs = (
        P(("vp", "vc"), None),
        P(("vp", "vc"), None, None),
        P(("vp", "vc"), None),
        P(("vp", "vc")),
    )
    return jax.shard_map(
        per_device, mesh=mesh, in_specs=in_specs, out_specs=P("vc", "vp"), check_vma=False
    )
```

```python
import jax
import jax.numpy as jnp
from jax import lax
from jax.experimental import pallas as pl
from jax.experimental.pallas import tpu as pltpu
from jax.sharding import PartitionSpec as P

TILE = 128
AB_TILES = 16
ROWS = 16
GROUP = 4
UNROLL = 4
FIRST = 79

SMEM = pl.BlockSpec(memory_space=pltpu.SMEM)
HBM = pl.BlockSpec(memory_space=pltpu.HBM)
VMEM = pl.BlockSpec(memory_space=pltpu.VMEM)


class Table:
    def __init__(self, slots):
        groups = slots // GROUP + AB_TILES + UNROLL
        self.entries = groups * GROUP
        self.c = 0
        self.s = self.entries
        self.a = 2 * self.entries
        self.n = self.a + groups
        self.other = self.n + 1
        self.dy = self.other + 8
        self.size = self.dy + 4
        self.groups = groups


def plan_kernel(columns, at, ab_ref, cd_ref, count_ref, p_ref, v_ref, tiles_hbm, t_ref, tiles, next_ref, sem):
    copy = pltpu.make_async_copy(tiles_hbm, tiles, sem)
    copy.start()
    live = count_ref[0]
    p, v = p_ref[0], v_ref[0]
    for k in range(8):
        t_ref[at.other + k] = ((p + k) % 8 // 4 + v) % 2
    for k in range(4):
        t_ref[at.dy + k] = (p // 8 + k - v // 2 + 4) % 4
    for k in range(AB_TILES):
        next_ref[k] = 0

    def count(i, _):
        a = ab_ref[i]
        next_ref[a] = next_ref[a] + 1
        return 0

    lax.fori_loop(0, live, count, 0)

    def blank(i, _):
        for k in range(8):
            t_ref[at.c + i * 8 + k] = columns
            t_ref[at.s + i * 8 + k] = 0
        return 0

    lax.fori_loop(0, at.entries // 8, blank, 0)
    for k in range(at.groups):
        t_ref[at.a + k] = 0

    def place(a, first):
        n = (next_ref[a] + GROUP - 1) // GROUP
        next_ref[a] = first * GROUP

        def mark(g, _):
            t_ref[at.a + first + g] = a
            return 0

        lax.fori_loop(0, n, mark, 0)
        return first + n

    t_ref[at.n] = (lax.fori_loop(0, AB_TILES, place, 0) + UNROLL - 1) // UNROLL

    def fill(i, _):
        a = ab_ref[i]
        e = next_ref[a]
        t_ref[at.c + e] = cd_ref[i]
        t_ref[at.s + e] = i
        next_ref[a] = e + 1
        return 0

    lax.fori_loop(0, live, fill, 0)
    copy.wait()


def make_plan(ab, cd, count, p, v, tiles, columns):
    at = Table(ab.shape[0])
    return pl.pallas_call(
        lambda *refs: plan_kernel(columns, at, *refs),
        out_shape=(jax.ShapeDtypeStruct((at.size,), jnp.int32), pltpu.VMEM(tiles.shape, tiles.dtype)),
        in_specs=[SMEM] * 5 + [HBM],
        out_specs=(SMEM, VMEM),
        scratch_shapes=[pltpu.SMEM((AB_TILES,), jnp.int32), pltpu.SemaphoreType.DMA],
        compiler_params=pltpu.CompilerParams(vmem_limit_bytes=1024 * 1024),
        name="plan",
    )(ab, cd, count, p.reshape(1), v.reshape(1), tiles)


def contract_kernel(spots, pieces, carried, n_arrays, at, t_ref, *refs):
    arrays = refs[:n_arrays]
    tiles = refs[n_arrays]
    refs = refs[n_arrays + 1 + carried :]
    outs, (rows, acc, sems) = refs[:-3], refs[-3:]
    columns = rows.shape[1] - 1
    for array, offset, first, depth, k in pieces:
        pltpu.make_async_copy(
            arrays[array].at[pl.ds(offset, depth)], rows.at[k, pl.ds(first, depth)], sems.at[0]
        ).start()
    for k in range(len(spots)):
        rows[k, columns] = jnp.zeros((ROWS, TILE), rows.dtype)

    def clear(i, _):
        acc[pl.ds(pl.multiple_of(i * ROWS, ROWS), ROWS), :] = jnp.zeros(
            (ROWS, acc.shape[1]), jnp.float32
        )
        return 0

    lax.fori_loop(0, len(spots), clear, 0)
    filled = rows.at[:, pl.ds(0, columns)]
    pltpu.make_async_copy(filled, filled, sems.at[0]).wait()

    def step(i, _):
        sums = []
        for u in range(UNROLL):
            e = (i * UNROLL + u) * GROUP
            cs = [t_ref[at.c + e + j] for j in range(GROUP)]
            lhs = jnp.concatenate(
                [
                    jnp.concatenate([rows[k, c] for k in range(len(spots))], axis=0)
                    for c in cs
                ],
                axis=1,
            )
            rhs = jnp.concatenate([tiles[t_ref[at.s + e + j]] for j in range(GROUP)], axis=0)
            sums.append(jnp.dot(lhs, rhs, preferred_element_type=jnp.float32))
        for u in range(UNROLL):
            a = t_ref[at.a + i * UNROLL + u]
            acc[:, pl.ds(pl.multiple_of(a * TILE, TILE), TILE)] += sums[u]
        return 0

    lax.fori_loop(0, t_ref[at.n], step, 0)

    for k, (dx, dz, out, index) in enumerate(spots):
        dy = t_ref[at.dy + dx]
        for side in range(2):

            @pl.when(t_ref[at.other + dz] == side)
            def _():
                pltpu.make_async_copy(
                    acc.at[pl.ds(k * ROWS, ROWS)], outs[2 * out + side].at[dy, index], sems.at[1]
                ).start()

    pltpu.make_async_copy(acc, acc, sems.at[1]).wait()


def contract(wanted, out_depths, held, carried, tiles, plan):
    arrays, pieces = [], []
    for k, (dx, dz, _, _) in enumerate(wanted):
        for array, offset, first, depth in held[dx % 4, dz % 8]:
            found = [i for i, a in enumerate(arrays) if a is array]
            if not found:
                arrays.append(array)
                found = [len(arrays) - 1]
            pieces.append((found[0], offset, first, depth, k))
    columns = sum(p[3] for p in pieces) // len(wanted)
    spots = [(dx % 4, dz % 8, out, index) for dx, dz, out, index in wanted]
    slots = tiles.shape[0]
    at = Table(slots)
    width = AB_TILES * TILE
    height = ROWS * len(spots)
    shapes = [
        jax.ShapeDtypeStruct((4, depth, ROWS, width), jnp.float32) for depth in out_depths for _ in range(2)
    ]
    return pl.pallas_call(
        lambda *refs: contract_kernel(spots, pieces, len(carried), len(arrays), at, *refs),
        out_shape=tuple(shapes),
        in_specs=[SMEM] + [HBM] * len(arrays) + [VMEM] + [HBM] * len(carried),
        out_specs=(HBM,) * len(shapes),
        scratch_shapes=[
            pltpu.VMEM((len(spots), columns + 1, ROWS, TILE), tiles.dtype),
            pltpu.VMEM((height, width), jnp.float32),
            pltpu.SemaphoreType.DMA((2,)),
        ],
        input_output_aliases={2 + len(arrays) + i: i for i in range(len(carried))},
        compiler_params=pltpu.CompilerParams(vmem_limit_bytes=9 * 1024 * 1024),
        cost_estimate=pl.CostEstimate(
            flops=2 * height * slots * TILE * TILE,
            bytes_accessed=2 * height * columns * TILE + 2 * slots * TILE * TILE + 4 * height * width,
            transcendentals=0,
        ),
        name="contract",
    )(plan, *arrays, tiles, *carried)


XP = [(p, (p + 8) % 32) for p in range(32)]
XM = [(b, a) for a, b in XP]
ZP = [(p, p // 8 * 8 + (p + 1) % 8) for p in range(32)]
ZM = [(b, a) for a, b in ZP]
CX = [(v, v ^ 1) for v in range(8)]
YP = [(v, (v + 2) % 8) for v in range(8)]
YM = [(b, a) for a, b in YP]
YY = [(v, (v + 4) % 8) for v in range(8)]


def send(value, perm, axis="vp"):
    return lax.ppermute(value, axis, perm)


def scatter_core(keep, moved):
    got = send(moved, CX, "vc")
    return [keep[k] + got[k] for k in range(4)]


def scatter_y(part):
    plus = send(part[1], YP, "vc")
    minus = send(part[3], YM, "vc")
    far = send(part[2], YY, "vc")
    return (part[0] + plus + minus + far).astype(jnp.bfloat16)


def scatter_ring(part):
    mine, plus, far, minus = part
    far_p = send(far[:1], YP, "vc")
    far_m = send(far[1:], YM, "vc")
    plus = jnp.concatenate([plus[:1] + far_p, plus[1:]], axis=0)
    minus = jnp.concatenate([minus[:1], minus[1:] + far_m], axis=0)
    plus = send(plus, YP, "vc")
    minus = send(minus, YM, "vc")
    return (mine + plus + minus).astype(jnp.bfloat16)


def body(amplitudes, pair_tiles, slot_pairs, slot_count):
    mixed = lax.all_to_all(amplitudes, "vc", split_axis=1, concat_axis=0, tiled=True)
    columns = mixed.shape[1] // TILE
    block = mixed.reshape(ROWS, columns, TILE).swapaxes(0, 1)
    a, b = FIRST, columns - FIRST
    p, v = lax.axis_index("vp"), lax.axis_index("vc")
    held = {(dx, dz): [] for dx in range(4) for dz in range(8)}
    xs = [0, -1, 1, 2]

    def both(pair, perms):
        return send(pair[0], perms[0]), send(pair[1], perms[1])

    def on_x(g, plus, zs):
        near = both((g, g), (XP, XM))
        far = send(near[0], XP) if plus else send(near[1], XM)
        for i, z in enumerate(zs):
            for dx, array in ((-1, near[0]), (1, near[1]), (2, far)):
                held[dx % 4, z % 8].append((array, i * b, a, b))

    def on_z(pair):
        return both(pair, (ZP, ZM))

    plan, tiles = make_plan(
        slot_pairs[:, 0], slot_pairs[:, 1], slot_count, p, v, pair_tiles, columns
    )

    xa = both((block, block), (XP, XM))
    own_b = block[a:]
    b1 = on_z((own_b, own_b))
    xf = both((xa[0][: a // 2], xa[1][a // 2 : a]), (XP, XM))
    xg = send(xa[0][a:], XP)
    four = jnp.concatenate([block[:a], xa[0][:a], xa[1][:a], xf[0], xf[1]], axis=0)
    b2 = on_z(b1)
    b3 = on_z(b2)
    b4 = send(b3[0], ZP)
    a1 = on_z((four, four))
    a2 = on_z(a1)
    a3 = on_z(a2)
    join = lambda pair: jnp.concatenate(pair, axis=0)
    on_x(join(b1), True, (-1, 1))
    on_x(join(b2), False, (-2, 2))
    on_x(join(b3), False, (-3, 3))
    on_x(b4, True, (4,))
    for k, pair in enumerate(((four, four), a1, a2, a3)):
        for at, dx in enumerate(xs):
            held[dx % 4, -k % 8].append((pair[0], at * a, 0, a))
            if k:
                held[dx % 4, k].append((pair[1], at * a, 0, a))
    held[0, 0].append((block, a, a, b))
    held[3, 0].append((xa[0], a, a, b))
    held[1, 0].append((xa[1], a, a, b))
    held[2, 0].append((xg, 0, a, b))
    for k, pair in ((1, b1), (2, b2), (3, b3)):
        held[0, 8 - k].append((pair[0], 0, a, b))
        held[0, k].append((pair[1], 0, a, b))
    held[0, 4].append((b4, 0, a, b))

    def run(sources, depths, carried):
        wanted = [(dx, dz, out, i) for dz, out, i in sources for dx in xs]
        return contract(wanted, depths, held, carried, tiles, plan)

    even_keep, even_send = run(((0, 0, 0),), (1,), ())
    odd_keep, odd_send = run(((1, 0, 0), (-1, 0, 1)), (2,), ())
    two_keep, two_send = run(((2, 0, 0), (-2, 0, 0)), (1,), ())
    last = lax.optimization_barrier((*a3, two_keep))
    cut = 2 * a
    a4 = both((last[0][:cut], last[1][cut:]), (ZP, ZM))
    for at, dx in enumerate(xs):
        for array, lo, hi in ((a4[0], 0, cut), (a4[1], cut, 4 * a)):
            first, end = max(lo, at * a), min(hi, at * a + a)
            if first < end:
                held[dx % 4, 4].append((array, first - lo, first - at * a, end - first))
    two = scatter_core(two_keep, two_send)
    odd = scatter_core(*run(((-3, 0, 0), (3, 0, 1)), (2,), (odd_keep, odd_send)))
    even = scatter_core(*run(((4, 0, 0),), (1,), (even_keep, even_send)))
    two, odd, even = scatter_y(two), scatter_ring(odd), scatter_y(even)
    by_z = [two[0], odd[0], two[0], odd[1]]
    ring = jnp.concatenate(by_z + by_z[:3], axis=0)
    turned = lax.dynamic_slice_in_dim(ring, (4 - p % 4) % 4 * ROWS, 4 * ROWS, 0)
    return lax.dynamic_update_slice_in_dim(turned, even[0], p % 4 * ROWS, 0)


def solution(mesh):
    in_specs = (
        P(("vp", "vc"), None),
        P(("vp", "vc"), None, None),
        P(("vp", "vc"), None),
        P(("vp", "vc")),
    )
    return jax.shard_map(
        body, mesh=mesh, in_specs=in_specs, out_specs=P("vc", "vp"), check_vma=False
    )
```

```python
import jax
import jax.numpy as jnp
from jax import lax
from jax.experimental import pallas as pl
from jax.experimental.pallas import tpu as pltpu
from jax.sharding import PartitionSpec as P

TILE = 128
AB_TILES = 16
ROWS = 16
GROUP = 4
UNROLL = 4
FIRST = 78

SMEM = pl.BlockSpec(memory_space=pltpu.SMEM)
HBM = pl.BlockSpec(memory_space=pltpu.HBM)
VMEM = pl.BlockSpec(memory_space=pltpu.VMEM)


class Table:
    def __init__(self, slots):
        groups = slots // GROUP + AB_TILES + UNROLL
        self.entries = groups * GROUP
        self.c = 0
        self.s = self.entries
        self.a = 2 * self.entries
        self.n = self.a + groups
        self.other = self.n + 1
        self.dy = self.other + 8
        self.size = self.dy + 4
        self.groups = groups


def plan_kernel(columns, at, ab_ref, cd_ref, count_ref, p_ref, v_ref, tiles_hbm, t_ref, tiles, next_ref, sem):
    copy = pltpu.make_async_copy(tiles_hbm, tiles, sem)
    copy.start()
    live = count_ref[0]
    p, v = p_ref[0], v_ref[0]
    for k in range(8):
        t_ref[at.other + k] = ((p + k) % 8 // 4 + v) % 2
    for k in range(4):
        t_ref[at.dy + k] = (p // 8 + k - v // 2 + 4) % 4
    for k in range(AB_TILES):
        next_ref[k] = 0

    def count(i, _):
        a = ab_ref[i]
        next_ref[a] = next_ref[a] + 1
        return 0

    lax.fori_loop(0, live, count, 0)

    def blank(i, _):
        for k in range(8):
            t_ref[at.c + i * 8 + k] = columns
            t_ref[at.s + i * 8 + k] = 0
        return 0

    lax.fori_loop(0, at.entries // 8, blank, 0)
    for k in range(at.groups):
        t_ref[at.a + k] = 0

    def place(a, first):
        n = (next_ref[a] + GROUP - 1) // GROUP
        next_ref[a] = first * GROUP

        def mark(g, _):
            t_ref[at.a + first + g] = a
            return 0

        lax.fori_loop(0, n, mark, 0)
        return first + n

    t_ref[at.n] = (lax.fori_loop(0, AB_TILES, place, 0) + UNROLL - 1) // UNROLL

    def fill(i, _):
        a = ab_ref[i]
        e = next_ref[a]
        t_ref[at.c + e] = cd_ref[i]
        t_ref[at.s + e] = i
        next_ref[a] = e + 1
        return 0

    lax.fori_loop(0, live, fill, 0)
    copy.wait()


def make_plan(ab, cd, count, p, v, tiles, columns):
    at = Table(ab.shape[0])
    return pl.pallas_call(
        lambda *refs: plan_kernel(columns, at, *refs),
        out_shape=(jax.ShapeDtypeStruct((at.size,), jnp.int32), pltpu.VMEM(tiles.shape, tiles.dtype)),
        in_specs=[SMEM] * 5 + [HBM],
        out_specs=(SMEM, VMEM),
        scratch_shapes=[pltpu.SMEM((AB_TILES,), jnp.int32), pltpu.SemaphoreType.DMA],
        compiler_params=pltpu.CompilerParams(vmem_limit_bytes=1024 * 1024),
        name="plan",
    )(ab, cd, count, p.reshape(1), v.reshape(1), tiles)


def load_kernel(source, target, sem):
    copy = pltpu.make_async_copy(source, target, sem)
    copy.start()
    copy.wait()


def load_tiles(tiles):
    return pl.pallas_call(
        load_kernel,
        out_shape=pltpu.VMEM(tiles.shape, tiles.dtype),
        in_specs=[HBM],
        out_specs=VMEM,
        scratch_shapes=[pltpu.SemaphoreType.DMA],
        compiler_params=pltpu.CompilerParams(vmem_limit_bytes=1024 * 1024),
        name="load",
    )(tiles)


def contract_kernel(spots, pieces, carried, n_arrays, at, unroll, t_ref, *refs):
    arrays = refs[:n_arrays]
    tiles = refs[n_arrays]
    refs = refs[n_arrays + 1 + carried :]
    outs, (rows, acc, sems) = refs[:-3], refs[-3:]
    columns = rows.shape[1] - 1
    for array, offset, first, depth, k in pieces:
        pltpu.make_async_copy(
            arrays[array].at[pl.ds(offset, depth)], rows.at[k, pl.ds(first, depth)], sems.at[0]
        ).start()
    for k in range(len(spots)):
        rows[k, columns] = jnp.zeros((ROWS, TILE), rows.dtype)

    def clear(i, _):
        acc[pl.ds(pl.multiple_of(i * ROWS, ROWS), ROWS), :] = jnp.zeros(
            (ROWS, acc.shape[1]), jnp.float32
        )
        return 0

    lax.fori_loop(0, len(spots), clear, 0)
    filled = rows.at[:, pl.ds(0, columns)]
    pltpu.make_async_copy(filled, filled, sems.at[0]).wait()

    def step(i, _):
        sums = []
        for u in range(unroll):
            e = (i * unroll + u) * GROUP
            cs = [t_ref[at.c + e + j] for j in range(GROUP)]
            lhs = jnp.concatenate(
                [
                    jnp.concatenate([rows[k, c] for k in range(len(spots))], axis=0)
                    for c in cs
                ],
                axis=1,
            )
            rhs = jnp.concatenate([tiles[t_ref[at.s + e + j]] for j in range(GROUP)], axis=0)
            sums.append(jnp.dot(lhs, rhs, preferred_element_type=jnp.float32))
        for u in range(unroll):
            a = t_ref[at.a + i * unroll + u]
            acc[:, pl.ds(pl.multiple_of(a * TILE, TILE), TILE)] += sums[u]
        return 0

    lax.fori_loop(0, t_ref[at.n] * (UNROLL // unroll), step, 0)

    for first in range(0, len(spots), 4):
        _, dz, out, index = spots[first]

        def put(dx, _):
            at_row = pl.multiple_of((first + dx) * ROWS, ROWS)
            for side in range(2):

                @pl.when(t_ref[at.other + dz] == side)
                def _():
                    pltpu.make_async_copy(
                        acc.at[pl.ds(at_row, ROWS)],
                        outs[2 * out + side].at[t_ref[at.dy + dx], index],
                        sems.at[1],
                    ).start()

            return 0

        lax.fori_loop(0, 4, put, 0)

    pltpu.make_async_copy(acc, acc, sems.at[1]).wait()


def contract(wanted, out_depths, held, carried, tiles, plan, unroll):
    arrays, pieces = [], []
    for k, (dx, dz, _, _) in enumerate(wanted):
        for array, offset, first, depth in held[dx % 4, dz % 8]:
            found = [i for i, a in enumerate(arrays) if a is array]
            if not found:
                arrays.append(array)
                found = [len(arrays) - 1]
            pieces.append((found[0], offset, first, depth, k))
    columns = sum(p[3] for p in pieces) // len(wanted)
    spots = [(dx % 4, dz % 8, out, index) for dx, dz, out, index in wanted]
    slots = tiles.shape[0]
    at = Table(slots)
    width = AB_TILES * TILE
    height = ROWS * len(spots)
    shapes = [
        jax.ShapeDtypeStruct((4, depth, ROWS, width), jnp.float32) for depth in out_depths for _ in range(2)
    ]
    return pl.pallas_call(
        lambda *refs: contract_kernel(spots, pieces, len(carried), len(arrays), at, unroll, *refs),
        out_shape=tuple(shapes),
        in_specs=[SMEM] + [HBM] * len(arrays) + [VMEM] + [HBM] * len(carried),
        out_specs=(HBM,) * len(shapes),
        scratch_shapes=[
            pltpu.VMEM((len(spots), columns + 1, ROWS, TILE), tiles.dtype),
            pltpu.VMEM((height, width), jnp.float32),
            pltpu.SemaphoreType.DMA((2,)),
        ],
        input_output_aliases={2 + len(arrays) + i: i for i in range(len(carried))},
        compiler_params=pltpu.CompilerParams(vmem_limit_bytes=9 * 1024 * 1024),
        cost_estimate=pl.CostEstimate(
            flops=2 * height * slots * TILE * TILE,
            bytes_accessed=2 * height * columns * TILE + 2 * slots * TILE * TILE + 4 * height * width,
            transcendentals=0,
        ),
        name="contract",
    )(plan, *arrays, tiles, *carried)


XP = [(p, (p + 8) % 32) for p in range(32)]
XM = [(b, a) for a, b in XP]
ZP = [(p, p // 8 * 8 + (p + 1) % 8) for p in range(32)]
ZM = [(b, a) for a, b in ZP]
CX = [(v, v ^ 1) for v in range(8)]
YP = [(v, (v + 2) % 8) for v in range(8)]
YM = [(b, a) for a, b in YP]
YY = [(v, (v + 4) % 8) for v in range(8)]


def send(value, perm, axis="vp"):
    return lax.ppermute(value, axis, perm)


def scatter_core(keep, moved):
    got = send(moved, CX, "vc")
    return [keep[k] + got[k] for k in range(4)]


def scatter_y(part):
    plus = send(part[1], YP, "vc")
    minus = send(part[3], YM, "vc")
    far = send(part[2], YY, "vc")
    return (part[0] + plus + minus + far).astype(jnp.bfloat16)


def scatter_ring(part):
    mine, plus, far, minus = part
    far = send(far, YM, "vc")
    plus = send(plus, YP, "vc")
    minus = send(minus + far, YM, "vc")
    return (mine + plus + minus).astype(jnp.bfloat16)


def body(amplitudes, pair_tiles, slot_pairs, slot_count):
    mixed = lax.all_to_all(amplitudes, "vc", split_axis=1, concat_axis=0, tiled=True)
    columns = mixed.shape[1] // TILE
    block = mixed.reshape(ROWS, columns, TILE).swapaxes(0, 1)
    a, b = FIRST, columns - FIRST
    p, v = lax.axis_index("vp"), lax.axis_index("vc")
    held = {(dx, dz): [] for dx in range(4) for dz in range(8)}
    xs = [0, -1, 1, 2]

    def both(pair, perms):
        return send(pair[0], perms[0]), send(pair[1], perms[1])

    def on_x(g, plus, zs, more=()):
        near = both((g, g), (XP, XM))
        if more:
            far = send(jnp.concatenate([near[0], *more], axis=0), XP)
            held[2, 0].append((far, len(zs) * b, a, b))
        else:
            far = send(near[0], XP) if plus else send(near[1], XM)
        for i, z in enumerate(zs):
            for dx, array in ((-1, near[0]), (1, near[1]), (2, far)):
                held[dx % 4, z % 8].append((array, i * b, a, b))

    def on_z(pair):
        return both(pair, (ZP, ZM))

    plan, tiles = make_plan(
        slot_pairs[:, 0], slot_pairs[:, 1], slot_count, p, v, pair_tiles, columns
    )

    xa = both((block, block), (XP, XM))
    own_b = block[a:]
    b1 = on_z((own_b, own_b))
    xf = send(xa[0][:a], XP)
    four = jnp.concatenate([block[:a], xa[0][:a], xa[1][:a], xf], axis=0)
    b2 = on_z(b1)
    b3 = on_z(b2)
    b4 = send(b3[0], ZP)
    a1 = on_z((four, four))
    a2 = on_z(a1)
    a3 = on_z(a2)

    def join(pair):
        return jnp.concatenate(pair, axis=0)

    on_x(join(b1), True, (-1, 1), (xa[0][a:],))
    on_x(join(b2), False, (-2, 2))
    on_x(join(b3), False, (-3, 3))
    on_x(b4, True, (4,))
    for k, pair in enumerate(((four, four), a1, a2, a3)):
        for at, dx in enumerate(xs):
            held[dx % 4, -k % 8].append((pair[0], at * a, 0, a))
            if k:
                held[dx % 4, k].append((pair[1], at * a, 0, a))
    held[0, 0].append((block, a, a, b))
    held[3, 0].append((xa[0], a, a, b))
    held[1, 0].append((xa[1], a, a, b))
    for k, pair in ((1, b1), (2, b2), (3, b3)):
        held[0, 8 - k].append((pair[0], 0, a, b))
        held[0, k].append((pair[1], 0, a, b))
    held[0, 4].append((b4, 0, a, b))

    again = load_tiles(pair_tiles)

    def run(name, sources, depths, carried):
        wanted = [(dx, dz, out, i) for dz, out, i in sources for dx in range(4)]
        kept = again if name == "keven" else tiles
        unroll = UNROLL
        return contract(wanted, depths, held, carried, kept, plan, unroll)

    even_keep, even_send = run("kzero", ((0, 0, 0),), (1,), ())
    odd_keep, odd_send = run("kone", ((1, 0, 0), (-1, 0, 1)), (2,), ())
    two_keep, two_send = run("ktwo", ((2, 0, 0), (-2, 0, 0)), (1,), ())
    last = lax.optimization_barrier((*a3, two_keep))
    cut = 2 * a
    a4 = both((last[0][:cut], last[1][cut:]), (ZP, ZM))
    for at, dx in enumerate(xs):
        for array, lo, hi in ((a4[0], 0, cut), (a4[1], cut, 4 * a)):
            first, end = max(lo, at * a), min(hi, at * a + a)
            if first < end:
                held[dx % 4, 4].append((array, first - lo, first - at * a, end - first))
    two = scatter_core(two_keep, two_send)
    odd = scatter_core(*run("kodd", ((-3, 0, 0), (3, 0, 1)), (2,), (odd_keep, odd_send)))
    even = scatter_core(*run("keven", ((4, 0, 0),), (1,), (even_keep, even_send)))
    two, odd, even = scatter_y(two), scatter_ring(odd), scatter_y(even)
    two, odd = lax.optimization_barrier((two, odd))
    by_z = [two[0], odd[0], two[0], odd[1]]
    ring = jnp.concatenate(by_z + by_z[:3], axis=0)
    turned = lax.dynamic_slice_in_dim(ring, (4 - p % 4) % 4 * ROWS, 4 * ROWS, 0)
    return lax.dynamic_update_slice_in_dim(turned, even[0], p % 4 * ROWS, 0)


def solution(mesh):
    in_specs = (
        P(("vp", "vc"), None),
        P(("vp", "vc"), None, None),
        P(("vp", "vc"), None),
        P(("vp", "vc")),
    )
    return jax.shard_map(
        body, mesh=mesh, in_specs=in_specs, out_specs=P("vc", "vp"), check_vma=False
    )
```
